32 devices in a mesh: replica: 8 (over z, y), shard: 4 (over x, core).
Axes of the slice: x: 2, y: 2, z: 4, core: 2. Of those that a mesh axis runs over, the one named last changes fastest.
Arguments:
- tokens: bfloat16 [12288, 1536], P(('replica', 'shard')), may hold values from -6 to 6
- query_weight: bfloat16 [1536, 1536], P('shard'), may hold values from -0.15625 to 0.15625
- key_weight: bfloat16 [1536, 512], P('shard'), may hold values from -0.15625 to 0.15625
- value_weight: bfloat16 [1536, 512], P('shard'), may hold values from -0.15625 to 0.15625
- output_weight: bfloat16 [1536, 1536], P('shard'), may hold values from -2 to 2
- attn_gain: bfloat16 [1536], P('shard'), may hold values from 0.5 to 1.5
- moe_gain: bfloat16 [1536], P('shard'), may hold values from 0.5 to 1.5
- gate_weight: bfloat16 [8, 1536, 512], P('shard'), may hold values from -0.15625 to 0.15625
- up_weight: bfloat16 [8, 1536, 512], P('shard'), may hold values from -0.15625 to 0.15625
- down_weight: bfloat16 [8, 512, 1536], P('shard'), may hold values from -1 to 1
- routes: int32 [12288, 4], P(('replica', 'shard')), may hold values from 0 to 7, all different within a row; in each aligned block of 384 rows (0 to 383, 384 to 767, ...) at most 256 rows name the same one
- route_probs: float32 [12288, 4], P(('replica', 'shard')), may hold values from 0.02 to 0.25
- cotangent: bfloat16 [12288, 1536], P(('replica', 'shard')), may hold values from -6 to 6
Outputs:
- mixed: bfloat16 [12288, 1536], P(('replica', 'shard'))
- tokens_grad: bfloat16 [12288, 1536], P(('replica', 'shard'))
- query_grad: float32 [1536, 1536], P('shard')
- key_grad: float32 [1536, 512], P('shard')
- value_grad: float32 [1536, 512], P('shard')
- output_grad: float32 [1536, 1536], P('shard')
- attn_gain_grad: float32 [1536], P('shard')
- moe_gain_grad: float32 [1536], P('shard')
- gate_grad: float32 [8, 1536, 512], P('shard')
- up_grad: float32 [8, 1536, 512], P('shard')
- down_grad: float32 [8, 512, 1536], P('shard')
The draws below stay inside these ranges and needn't reach their ends.
Inputs may be any that keep to these rules, and one draw needn't show every extreme that they name: `routes`: in the 384 rows of one sequence no expert is named by more than 256 (token, choice) pairs; a row names 4 different experts.
All inputs are finite; a program needn't handle non-finite values.
Results may differ from the reference program's by a relative error of at most 0.019.
Values may be sent and summed in bfloat16 or wider, within the bound.
No kernel may reach another device: no remote copies, remote signals or barrier semaphores. Data moves between devices by JAX's collectives and lax.ppermute only.
A program may use at most 384 MiB of HBM per device.

```python
import math
import jax
import jax.numpy as jnp
import numpy as np
from jax import lax

D = 1536
HEADS = 24
KV_HEADS = 8
HEAD_DIM = 64
EXPERTS = 8
EXPERT_FF = 512
TOP_K = 4
LEN = 384
CAPACITY = 256
TOKENS = 12288


def block_scale(key, extent, split, smallest, top_value):
    def one(dim, blocks):
        draws = jax.random.uniform(jax.random.fold_in(jax.random.fold_in(key, 6), dim), (blocks,), jnp.float32, smallest / len(split), top_value / len(split))
        return jnp.repeat(jnp.exp(draws), extent[dim] // blocks).reshape((-1,) + (1,) * (len(extent) - dim - 1))

    gain = one(*split[0])
    for cut in split[1:]:
        gain = gain * one(*cut)
    return gain


def deal_out(own_key, own, number, rows, number_of, top, most, lean):
    ranking = jax.random.permutation(own_key, number_of)
    heavy_load, ordinary = shares(number_of, rows * top, most, lean, True), shares(number_of, rows * top, most, lean, False)
    places = jnp.arange(number_of)

    def named(lengths, turn):
        used = int((lengths > 0).sum())
        fixed = max(1, used // 4)
        shifted = fixed + (places - fixed + turn * (used - fixed)) % max(1, number_of - fixed)
        return jnp.zeros((number_of,), jnp.int32).at[ranking[jnp.where(places < fixed, places, shifted)]].set(jnp.asarray(lengths, jnp.int32))

    lengths = jnp.where(number % 4 == 0, named(heavy_load, number // 4), named(ordinary, number - number // 4 - 1))
    mixed = jax.random.permutation(jax.random.fold_in(own, 3), number_of)
    source_of, receiver = mixed[0:number_of // 2 * 2:2], mixed[1:number_of // 2 * 2:2]
    margin = jnp.minimum(lengths[source_of] - 1, most - lengths[receiver]) // 2
    margin = jnp.where((source_of == ranking[0]) | (receiver == ranking[0]) | (lengths[receiver] == 0), 0, jnp.maximum(margin, 0))
    shifted = jax.random.randint(jax.random.fold_in(own, 4), (number_of // 2,), 0, 1 << 20) % (margin + 1)
    lengths = lengths.at[source_of].add(-shifted).at[receiver].add(shifted)
    labels = jnp.searchsorted(jnp.cumsum(lengths), jnp.arange(rows * top), side="right").astype(jnp.int32)
    table = labels.reshape(top, rows).T
    table = table[jax.random.permutation(jax.random.fold_in(own, 1), rows)]
    turn = jax.random.randint(jax.random.fold_in(own, 2), (rows, 1), 0, top)
    return jnp.take_along_axis(table, (jnp.arange(top)[None, :] + turn) % top, axis=1)


def shares(amount, total, reach, skew, full):
    loads = [(1 << 20) // math.isqrt(standing ** skew) + 1 for standing in range(1, amount + 1)]
    largest = reach if full else min(reach, max(-(-total // amount), total * loads[0] // sum(loads)))
    least = 1 if total - largest >= amount - 1 else 0
    holding, spare = [largest] + [least] * (amount - 1), total - largest - least * (amount - 1)
    while spare > 0:
        movable = [i for i in range(1, amount) if holding[i] < largest] or [i for i in range(1, amount) if holding[i] < reach]
        pool, budget = sum([loads[i] for i in movable]), spare
        for i in movable:
            extra = min(reach - holding[i], max(1, budget * loads[i] // pool), spare)
            holding[i] = holding[i] + extra
            spare = spare - extra
    return np.array(holding)


def centred(rng, dims, width, most, cuts=(), kind=jnp.bfloat16):
    values = width * jax.random.normal(rng, dims, jnp.float32)
    if cuts:
        values = values * block_scale(rng, dims, cuts, -0.22, 0.18)
    return jnp.clip(values, -most, most).astype(kind)


def setup_inputs(seed: int = 0) -> dict:
    keys = jax.random.split(jax.random.key(seed), 14)
    tokens = centred(keys[0], (TOKENS, D), 1.0, 6.0, ((0, 32),))
    query_weight = centred(keys[1], (D, HEADS * HEAD_DIM), D ** -0.5, 0.15625, ((0, 4),))
    key_weight = centred(keys[2], (D, KV_HEADS * HEAD_DIM), D ** -0.5, 0.15625, ((0, 4),))
    value_weight = centred(keys[3], (D, KV_HEADS * HEAD_DIM), D ** -0.5, 0.15625, ((0, 4),))
    output_weight = centred(keys[4], (HEADS * HEAD_DIM, D), (HEAD_DIM // 8) ** -0.5, 2.0, ((0, 4),))
    attn_gain = jnp.clip(1.0 + 0.1 * jax.random.normal(keys[5], (D,), jnp.float32), 0.5, 1.5).astype(jnp.bfloat16)
    moe_gain = jnp.clip(1.0 + 0.1 * jax.random.normal(keys[6], (D,), jnp.float32), 0.5, 1.5).astype(jnp.bfloat16)
    gate_weight = centred(keys[7], (EXPERTS, D, EXPERT_FF), D ** -0.5, 0.15625, ((0, 4),))
    up_weight = centred(keys[8], (EXPERTS, D, EXPERT_FF), D ** -0.5, 0.15625, ((0, 4),))
    down_weight = centred(keys[9], (EXPERTS, EXPERT_FF, D), (EXPERT_FF // 16) ** -0.5, 1.0, ((0, 4),))
    routes_keys = jax.random.split(jax.random.fold_in(keys[10], 1), TOKENS // LEN)
    routes_turns = jax.random.permutation(jax.random.fold_in(keys[10], 3), TOKENS // LEN)
    routes = jax.vmap(lambda own, number: deal_out(jax.random.fold_in(keys[10], 2), own, number, LEN, EXPERTS, TOP_K, CAPACITY, 1))(routes_keys, routes_turns).reshape((TOKENS, TOP_K))
    route_probs = jnp.clip(jnp.exp(math.log(0.25) - 2.5257287 * jax.random.uniform(keys[11], (TOKENS, TOP_K), jnp.float32) ** block_scale(keys[11], (TOKENS, TOP_K), ((0, 32),), -0.2, 0.2)), 0.02, 0.25)
    cotangent = centred(keys[12], (TOKENS, D), 1.0, 6.0, ((0, 32),))
    return {"tokens": tokens, "query_weight": query_weight, "key_weight": key_weight, "value_weight": value_weight, "output_weight": output_weight, "attn_gain": attn_gain, "moe_gain": moe_gain, "gate_weight": gate_weight, "up_weight": up_weight, "down_weight": down_weight, "routes": routes, "route_probs": route_probs, "cotangent": cotangent}


EPSILON = 1e-06
SCORE_SCALE = 0.015625
ROPE_BASE = 10000.0
NEGATIVE = -1e+30

def rope_tables(length):
    halfdim = HEAD_DIM // 2
    exponent = jnp.arange(halfdim, dtype=jnp.float32) * (2.0 / HEAD_DIM)
    inverse = ROPE_BASE ** (-exponent)
    angles = jnp.arange(length, dtype=jnp.float32)[:, None] * inverse[None, :]
    return (jnp.cos(angles), jnp.sin(angles))

def rotate(values, cosine, sine_vals, direction):
    halfdim = values.shape[-1] // 2
    lower_half = values[..., :halfdim]
    upper_half = values[..., halfdim:]
    cos_rows = cosine[:, None, :]
    sin_rows = sine_vals[:, None, :] * direction
    return jnp.concatenate([lower_half * cos_rows - upper_half * sin_rows, upper_half * cos_rows + lower_half * sin_rows], axis=-1)

def rms_forward(residual, gain_vec):
    inverse = lax.rsqrt(lax.optimization_barrier(jnp.mean(residual * residual, axis=-1, keepdims=True)) + EPSILON)
    scaled = residual * inverse
    return (scaled, inverse, (scaled * gain_vec.astype(jnp.float32)).astype(jnp.bfloat16))

def rms_backward(grad_normed, scaled, inverse, gain_vec):
    grad_scaled = grad_normed * gain_vec.astype(jnp.float32)
    gain_grad = lax.optimization_barrier(jnp.sum(grad_normed * scaled, axis=0))
    inner_mean = lax.optimization_barrier(jnp.mean(grad_scaled * scaled, axis=-1, keepdims=True))
    return (inverse * (grad_scaled - scaled * inner_mean), gain_grad)

def dispatch(routes, capacity):
    length, top_count = routes.shape
    flat_routes = routes.reshape(-1)
    onehot = (flat_routes[:, None] == jnp.arange(EXPERTS, dtype=jnp.int32)[None, :]).astype(jnp.int32)
    earlier = jnp.cumsum(onehot, axis=0) - onehot
    slot_rank = lax.optimization_barrier(jnp.sum(earlier * onehot, axis=1))
    slot_index = (flat_routes * capacity + slot_rank).astype(jnp.int32)
    token_ids = (jnp.arange(length * top_count, dtype=jnp.int32) // top_count).astype(jnp.int32)
    owners = jnp.zeros((EXPERTS * capacity,), jnp.int32).at[slot_index].set(token_ids)
    return (slot_index, owners)

def score_block(queries, keys_rot, allowed):
    raw_scores = jnp.einsum('qkgd,skd->kgqs', queries.astype(jnp.float32), keys_rot.astype(jnp.float32)) * SCORE_SCALE
    return jnp.where(allowed, raw_scores, NEGATIVE)

def sequence_pass(seq_tokens, seq_routes, seq_probs, seq_cotangent, weights):
    query_full, key_full, value_full, output_full, gain_one, gain_two, gate_full, up_full, down_full = weights
    f32 = jnp.float32
    bf16 = jnp.bfloat16
    length, model_width = seq_tokens.shape
    group_size = HEADS // KV_HEADS
    capacity = CAPACITY
    cosine, sine_vals = rope_tables(length)
    allowed = jnp.arange(length)[:, None] >= jnp.arange(length)[None, :]
    residual = seq_tokens.astype(f32)
    scaled_one, inverse_one, normed_one = rms_forward(residual, gain_one)
    query_pre = jnp.dot(normed_one, query_full, preferred_element_type=f32).reshape(length, HEADS, HEAD_DIM)
    queries = rotate(query_pre, cosine, sine_vals, 1.0).astype(bf16).reshape(length, KV_HEADS, group_size, HEAD_DIM)
    key_pre = jnp.dot(normed_one, key_full, preferred_element_type=f32).reshape(length, KV_HEADS, HEAD_DIM)
    keys_rot = rotate(key_pre, cosine, sine_vals, 1.0).astype(bf16)
    values = jnp.dot(normed_one, value_full, preferred_element_type=f32).astype(bf16).reshape(length, KV_HEADS, HEAD_DIM)
    scores = score_block(queries, keys_rot, allowed)
    row_max = lax.optimization_barrier(jnp.max(scores, axis=-1, keepdims=True))
    logsum = row_max + jnp.log(lax.optimization_barrier(jnp.sum(jnp.exp(scores - row_max), axis=-1, keepdims=True)))
    attn_probs = jnp.exp(scores - logsum).astype(bf16)
    attended = jnp.einsum('kgqs,skd->qkgd', attn_probs.astype(f32), values.astype(f32)).astype(bf16)
    attended_flat = attended.reshape(length, HEADS * HEAD_DIM)
    middle = residual + jnp.dot(attended_flat, output_full, preferred_element_type=f32)
    scaled_two, inverse_two, normed_two = rms_forward(middle, gain_two)
    slot_index, owners = dispatch(seq_routes, capacity)
    buffers = normed_two[owners].reshape(EXPERTS, capacity, model_width)
    buffers_f = buffers.astype(f32)
    gate_pre = jnp.einsum('ecd,edf->ecf', buffers_f, gate_full)
    up_pre = jnp.einsum('ecd,edf->ecf', buffers_f, up_full)
    hidden = (jax.nn.silu(gate_pre) * up_pre).astype(bf16)
    result = jnp.einsum('ecf,efd->ecd', hidden.astype(f32), down_full).astype(bf16)
    picked = result.reshape(EXPERTS * capacity, model_width)[slot_index].astype(f32).reshape(length, TOP_K, model_width)
    moe_out = lax.optimization_barrier(jnp.sum(picked * seq_probs[:, :, None], axis=1))
    mixed = (middle + moe_out).astype(bf16)
    grad_out = seq_cotangent.astype(f32)
    slot_grads = (seq_probs[:, :, None] * grad_out[:, None, :]).reshape(length * TOP_K, model_width)
    grad_result = jnp.zeros((EXPERTS * capacity, model_width), f32).at[slot_index].set(slot_grads).astype(bf16).reshape(EXPERTS, capacity, model_width)
    grad_result_f = grad_result.astype(f32)
    grad_hidden = jnp.einsum('ecd,efd->ecf', grad_result_f, down_full)
    down_g = jnp.einsum('ecf,ecd->efd', hidden.astype(f32), grad_result_f)
    sigmoid_vals = jax.nn.sigmoid(gate_pre)
    grad_up = (grad_hidden * gate_pre * sigmoid_vals).astype(bf16)
    grad_gate = (grad_hidden * up_pre * sigmoid_vals * (1.0 + gate_pre * (1.0 - sigmoid_vals))).astype(bf16)
    gate_g = jnp.einsum('ecd,ecf->edf', buffers_f, grad_gate.astype(f32))
    up_g = jnp.einsum('ecd,ecf->edf', buffers_f, grad_up.astype(f32))
    grad_buffers = (jnp.einsum('ecf,edf->ecd', grad_gate.astype(f32), gate_full) + jnp.einsum('ecf,edf->ecd', grad_up.astype(f32), up_full)).astype(bf16)
    grad_normed_two = lax.optimization_barrier(jnp.sum(grad_buffers.reshape(EXPERTS * capacity, model_width)[slot_index].astype(f32).reshape(length, TOP_K, model_width), axis=1))
    grad_back_two, gain_two_g = rms_backward(grad_normed_two, scaled_two, inverse_two, gain_two)
    grad_middle = grad_out + grad_back_two
    grad_mid_bf = grad_middle.astype(bf16)
    output_g = jnp.dot(attended_flat.T, grad_mid_bf, preferred_element_type=f32)
    grad_attended = jnp.dot(grad_mid_bf, output_full.T, preferred_element_type=f32).astype(bf16).reshape(length, KV_HEADS, group_size, HEAD_DIM)
    probs_full = jnp.exp(score_block(queries, keys_rot, allowed) - logsum)
    probs_bf = probs_full.astype(bf16)
    grad_values = jnp.einsum('kgqs,qkgd->skd', probs_bf.astype(f32), grad_attended.astype(f32)).astype(bf16)
    grad_probs = jnp.einsum('qkgd,skd->kgqs', grad_attended.astype(f32), values.astype(f32))
    delta_sum = lax.optimization_barrier(jnp.sum(grad_attended.astype(f32) * attended.astype(f32), axis=-1))
    delta_rows = jnp.transpose(delta_sum, (1, 2, 0))[..., None]
    grad_scores = (probs_full * (grad_probs - delta_rows) * SCORE_SCALE).astype(bf16)
    grad_query_rot = jnp.einsum('kgqs,skd->qkgd', grad_scores.astype(f32), keys_rot.astype(f32))
    grad_key_rot = jnp.einsum('kgqs,qkgd->skd', grad_scores.astype(f32), queries.astype(f32))
    grad_queries = rotate(grad_query_rot.reshape(length, HEADS, HEAD_DIM), cosine, sine_vals, -1.0).astype(bf16).reshape(length, HEADS * HEAD_DIM)
    grad_keys = rotate(grad_key_rot, cosine, sine_vals, -1.0).astype(bf16).reshape(length, KV_HEADS * HEAD_DIM)
    grad_values_flat = grad_values.reshape(length, KV_HEADS * HEAD_DIM)
    query_g = jnp.dot(normed_one.T, grad_queries, preferred_element_type=f32)
    key_g = jnp.dot(normed_one.T, grad_keys, preferred_element_type=f32)
    value_g = jnp.dot(normed_one.T, grad_values_flat, preferred_element_type=f32)
    grad_normed_one = jnp.dot(grad_queries, query_full.T, preferred_element_type=f32) + jnp.dot(grad_keys, key_full.T, preferred_element_type=f32) + jnp.dot(grad_values_flat, value_full.T, preferred_element_type=f32)
    grad_back_one, gain_one_g = rms_backward(grad_normed_one, scaled_one, inverse_one, gain_one)
    tokens_grad = (grad_middle + grad_back_one).astype(bf16)
    return (mixed, tokens_grad, (query_g, key_g, value_g, output_g, gain_one_g, gain_two_g, gate_g, up_g, down_g))

def reference(tokens, query_weight, key_weight, value_weight, output_weight, attn_gain, moe_gain, gate_weight, up_weight, down_weight, routes, route_probs, cotangent):
    model_width = tokens.shape[1]
    seq_count = tokens.shape[0] // LEN
    weights = (query_weight, key_weight, value_weight, output_weight, attn_gain, moe_gain, gate_weight.astype(jnp.float32), up_weight.astype(jnp.float32), down_weight.astype(jnp.float32))
    init = jax.tree.map(lambda array: jnp.zeros(array.shape, jnp.float32), (query_weight, key_weight, value_weight, output_weight, attn_gain, moe_gain, gate_weight, up_weight, down_weight))

    def step_fn(totals, seq_inputs):
        seq_tokens, seq_routes, seq_probs, seq_cotangent = seq_inputs
        mixed, tokens_grad, seq_grads = sequence_pass(seq_tokens, seq_routes, seq_probs, seq_cotangent, weights)
        return (jax.tree.map(jnp.add, totals, seq_grads), (mixed, tokens_grad))
    inputs_all = (tokens.reshape(seq_count, LEN, model_width), routes.reshape(seq_count, LEN, TOP_K), route_probs.reshape(seq_count, LEN, TOP_K), cotangent.reshape(seq_count, LEN, model_width))
    totals, (mixed_all, grads_all) = lax.scan(step_fn, init, inputs_all)
    return (mixed_all.reshape(-1, model_width), grads_all.reshape(-1, model_width), totals[0], totals[1], totals[2], totals[3], totals[4], totals[5], totals[6], totals[7], totals[8])
```

```python
import functools

import jax
import jax.numpy as jnp
from jax import lax
from jax.sharding import PartitionSpec as P

HEADS = 24
KV_HEADS = 8
HEAD_DIM = 64
EXPERTS = 8
TOP_K = 4


EPSILON = 1e-06
SCORE_SCALE = 0.015625
ROPE_BASE = 10000.0
NEGATIVE = -1e30


def rope_tables(length):
    halfdim = HEAD_DIM // 2
    exponent = jnp.arange(halfdim, dtype=jnp.float32) * (2.0 / HEAD_DIM)
    inverse = ROPE_BASE ** (-exponent)
    angles = jnp.arange(length, dtype=jnp.float32)[:, None] * inverse[None, :]
    return (jnp.cos(angles), jnp.sin(angles))


def rotate(values, cosine, sine_vals, direction):
    halfdim = values.shape[-1] // 2
    lower_half = values[..., :halfdim]
    upper_half = values[..., halfdim:]
    cos_rows = cosine[:, None, :]
    sin_rows = sine_vals[:, None, :] * direction
    return jnp.concatenate(
        [
            lower_half * cos_rows - upper_half * sin_rows,
            upper_half * cos_rows + lower_half * sin_rows,
        ],
        axis=-1,
    )


def rms_forward(residual, gain_vec):
    inverse = lax.rsqrt(jnp.mean(residual * residual, axis=-1, keepdims=True) + EPSILON)
    scaled = residual * inverse
    return (scaled, inverse, (scaled * gain_vec.astype(jnp.float32)).astype(jnp.bfloat16))


def rms_backward(grad_normed, scaled, inverse, gain_vec):
    grad_scaled = grad_normed * gain_vec.astype(jnp.float32)
    gain_grad = jnp.sum(grad_normed * scaled, axis=0)
    inner_mean = jnp.mean(grad_scaled * scaled, axis=-1, keepdims=True)
    return (inverse * (grad_scaled - scaled * inner_mean), gain_grad)


def score_block(queries, keys_rot, allowed):
    raw_scores = (
        jnp.einsum("qkgd,skd->kgqs", queries, keys_rot, preferred_element_type=jnp.float32)
        * SCORE_SCALE
    )
    return jnp.where(allowed, raw_scores, NEGATIVE)


def dot(a, b, dims):
    return lax.dot_general(a, b, (dims, ((), ())), preferred_element_type=jnp.float32)


def neighbour_core(value):
    return lax.ppermute(value, "shard", [(0, 1), (1, 0), (2, 3), (3, 2)])


def neighbour_x(value):
    return lax.ppermute(value, "shard", [(0, 2), (2, 0), (1, 3), (3, 1)])


def gather_parts(value):
    one = neighbour_core(value)
    two = neighbour_x(value)
    return (value, one, two, neighbour_core(two))


def scatter_parts(parts):
    near = add(parts[0], neighbour_core(parts[1]))
    far = add(parts[2], neighbour_core(parts[3]))
    return add(near, neighbour_x(far))


def add(a, b):
    return (a.astype(jnp.float32) + b.astype(jnp.float32)).astype(jnp.bfloat16)


def flip(value, bit, count):
    return lax.ppermute(value, "replica", [(i, i ^ bit) for i in range(count)])


def reduce_replicas(value, order, count):
    index = lax.axis_index("replica")
    for bit in order[:-1]:
        mine = jnp.minimum(index & bit, 1)
        halves = value.reshape((2, value.shape[0] // 2) + value.shape[1:])
        sent = lax.dynamic_index_in_dim(halves, 1 - mine, 0, keepdims=False)
        kept = lax.dynamic_index_in_dim(halves, mine, 0, keepdims=False)
        value = add(kept, flip(sent, bit, count))
    value = add(value, flip(value, order[-1], count))
    for bit in order[:-1][::-1]:
        mine = (index & bit) != 0
        other = flip(value, bit, count)
        value = jnp.concatenate(
            [jnp.where(mine, other, value), jnp.where(mine, value, other)], axis=0
        )
    return value


def body(
    count,
    tokens,
    query_weight,
    key_weight,
    value_weight,
    output_weight,
    attn_gain,
    moe_gain,
    gate_weight,
    up_weight,
    down_weight,
    routes,
    route_probs,
    cotangent,
):
    f32 = jnp.float32
    bf16 = jnp.bfloat16
    length, model_width = tokens.shape
    group_size = HEADS // KV_HEADS
    capacity = length * 2 // 3
    own = lax.axis_index("shard")
    chunk = query_weight.shape[0]
    held = gate_weight.shape[0]
    bits = []
    bit = 1
    while bit < count:
        bits.append(bit)
        bit *= 2
    orders = (tuple(bits), tuple([bits[1], bits[0]] + bits[2:]))

    def column_chunks(value):
        return tuple(
            lax.dynamic_slice_in_dim(value, (own ^ j) * chunk, chunk, 1) for j in range(4)
        )

    qkv_own = jnp.concatenate([query_weight, key_weight, value_weight], axis=1)
    gains_own = jnp.stack([attn_gain, moe_gain])
    gain_parts = gather_parts(gains_own)
    qkv_parts = gather_parts(qkv_own)
    output_parts = gather_parts(output_weight)
    grad_out_parts = gather_parts(cotangent)

    def natural(parts, axis):
        stacked = jnp.stack(parts)
        ordered = [lax.dynamic_index_in_dim(stacked, own ^ j, 0, keepdims=False) for j in range(4)]
        return jnp.concatenate(ordered, axis=axis)

    gains = natural(gain_parts, 1)
    gain_one, gain_two = gains[0], gains[1]

    expert_ids = jnp.arange(EXPERTS, dtype=jnp.int32)
    named = routes[:, :, None] == expert_ids[None, None, :]
    taken = jnp.any(named, axis=1)
    prob_of = jnp.sum(jnp.where(named, route_probs[:, :, None], 0.0), axis=1)
    positions = jnp.arange(length)
    before = (positions[:, None] > positions[None, :]).astype(bf16)
    slot_of = jnp.where(taken, dot(before, taken.astype(bf16), ((1,), (0,))), -1.0)
    info_own = jnp.concatenate([slot_of, prob_of], axis=1).T
    info_parts = gather_parts(info_own)

    cosine, sine_vals = rope_tables(length)
    allowed = positions[:, None] >= positions[None, :]
    residual = tokens.astype(f32)
    scaled_one, inverse_one, normed_one = rms_forward(residual, gain_one)
    normed_chunks = column_chunks(normed_one)
    qkv_pre = sum(dot(normed_chunks[j], qkv_parts[j], ((1,), (0,))) for j in range(4))
    heads_width = HEADS * HEAD_DIM
    kv_width = KV_HEADS * HEAD_DIM
    query_pre = qkv_pre[:, :heads_width].reshape(length, HEADS, HEAD_DIM)
    queries = (
        rotate(query_pre, cosine, sine_vals, 1.0)
        .astype(bf16)
        .reshape(length, KV_HEADS, group_size, HEAD_DIM)
    )
    key_pre = qkv_pre[:, heads_width : heads_width + kv_width].reshape(length, KV_HEADS, HEAD_DIM)
    keys_rot = rotate(key_pre, cosine, sine_vals, 1.0).astype(bf16)
    values = qkv_pre[:, heads_width + kv_width :].astype(bf16).reshape(length, KV_HEADS, HEAD_DIM)
    scores = score_block(queries, keys_rot, allowed)
    row_max = jnp.max(scores, axis=-1, keepdims=True)
    logsum = row_max + jnp.log(jnp.sum(jnp.exp(scores - row_max), axis=-1, keepdims=True))
    attn_probs = jnp.exp(scores - logsum).astype(bf16)
    attended = jnp.einsum("kgqs,skd->qkgd", attn_probs, values, preferred_element_type=f32).astype(
        bf16
    )
    attended_flat = attended.reshape(length, heads_width)
    attended_chunks = column_chunks(attended_flat)
    middle = residual + sum(
        dot(attended_chunks[j], output_parts[j], ((1,), (0,))) for j in range(4)
    )
    scaled_two, inverse_two, normed_two = rms_forward(middle, gain_two)

    normed_parts = gather_parts(normed_two)

    slots = jnp.arange(capacity, dtype=f32)

    def experts(pair):
        normed = jnp.stack([normed_parts[j] for j in pair])
        grads = jnp.stack([grad_out_parts[j] for j in pair])
        info = jnp.stack([info_parts[j] for j in pair])
        slot = lax.dynamic_slice_in_dim(info, own * held, held, 1)
        prob = lax.dynamic_slice_in_dim(info, EXPERTS + own * held, held, 1)
        pick = slot[:, :, None, :] == slots[None, None, :, None]
        slot_prob = jnp.sum(jnp.where(pick, prob[:, :, None, :], 0.0), axis=-1)[..., None]
        pick = pick.astype(bf16)
        buffers = jnp.einsum("qect,qtd->eqcd", pick, normed, preferred_element_type=f32).astype(bf16)
        slot_prob = jnp.transpose(slot_prob, (1, 0, 2, 3))
        grad_result = (
            jnp.einsum("qect,qtd->eqcd", pick, grads, preferred_element_type=f32) * slot_prob
        ).astype(bf16)
        gate_pre = jnp.einsum("eqcd,edf->eqcf", buffers, gate_weight, preferred_element_type=f32)
        up_pre = jnp.einsum("eqcd,edf->eqcf", buffers, up_weight, preferred_element_type=f32)
        sigmoid_vals = jax.nn.sigmoid(gate_pre)
        hidden = (gate_pre * sigmoid_vals * up_pre).astype(bf16)
        result = (
            jnp.einsum("eqcf,efd->eqcd", hidden, down_weight, preferred_element_type=f32)
            * slot_prob
        ).astype(bf16)
        moe_part = jnp.einsum("qect,eqcd->qtd", pick, result, preferred_element_type=f32).astype(
            bf16
        )
        grad_hidden = jnp.einsum(
            "eqcd,efd->eqcf", grad_result, down_weight, preferred_element_type=f32
        )
        grad_up = (grad_hidden * gate_pre * sigmoid_vals).astype(bf16)
        grad_gate = (
            grad_hidden * up_pre * sigmoid_vals * (1.0 + gate_pre * (1.0 - sigmoid_vals))
        ).astype(bf16)
        grad_buffers = (
            jnp.einsum("eqcf,edf->eqcd", grad_gate, gate_weight, preferred_element_type=f32)
            + jnp.einsum("eqcf,edf->eqcd", grad_up, up_weight, preferred_element_type=f32)
        ).astype(bf16)
        grad_part = jnp.einsum(
            "qect,eqcd->qtd", pick, grad_buffers, preferred_element_type=f32
        ).astype(bf16)
        return (buffers, grad_result, hidden, grad_gate, grad_up, moe_part, grad_part)

    near = experts((0, 1))
    far = experts((2, 3))
    grad_normed_two = scatter_parts(
        (near[6][0], near[6][1], far[6][0], far[6][1])
    ).astype(f32)
    moe_out = scatter_parts((near[5][0], near[5][1], far[5][0], far[5][1]))
    mixed = (middle + moe_out.astype(f32)).astype(bf16)

    def weight_grad(left, right):
        return (
            jnp.einsum("eqci,eqco->eio", near[left], near[right], preferred_element_type=f32)
            + jnp.einsum("eqci,eqco->eio", far[left], far[right], preferred_element_type=f32)
        ).astype(bf16)

    def summed(value, order):
        flat = value.reshape(-1, value.shape[-1])
        return reduce_replicas(flat, order, count).astype(f32).reshape(value.shape)

    down_g = summed(weight_grad(2, 1), orders[0])
    gate_g = summed(weight_grad(0, 3), orders[1])
    up_g = summed(weight_grad(0, 4), orders[0])

    grad_out = cotangent.astype(f32)
    grad_back_two, gain_two_g = rms_backward(grad_normed_two, scaled_two, inverse_two, gain_two)
    grad_middle = grad_out + grad_back_two
    grad_mid_bf = grad_middle.astype(bf16)
    output_g = scatter_parts(
        tuple(
            dot(attended_chunks[j], grad_mid_bf, ((0,), (0,))).astype(bf16) for j in range(4)
        )
    )
    output_g = summed(output_g, orders[1])
    grad_att_parts = tuple(
        dot(grad_mid_bf, output_parts[j], ((1,), (1,))).astype(bf16) for j in range(4)
    )
    grad_attended = natural(grad_att_parts, 1).reshape(length, KV_HEADS, group_size, HEAD_DIM)
    probs_full = jnp.exp(score_block(queries, keys_rot, allowed) - logsum)
    probs_bf = probs_full.astype(bf16)
    grad_values = jnp.einsum(
        "kgqs,qkgd->skd", probs_bf, grad_attended, preferred_element_type=f32
    ).astype(bf16)
    grad_probs = jnp.einsum("qkgd,skd->kgqs", grad_attended, values, preferred_element_type=f32)
    delta_sum = jnp.sum(grad_attended.astype(f32) * attended.astype(f32), axis=-1)
    delta_rows = jnp.transpose(delta_sum, (1, 2, 0))[..., None]
    grad_scores = (probs_full * (grad_probs - delta_rows) * SCORE_SCALE).astype(bf16)
    grad_query_rot = jnp.einsum("kgqs,skd->qkgd", grad_scores, keys_rot, preferred_element_type=f32)
    grad_key_rot = jnp.einsum("kgqs,qkgd->skd", grad_scores, queries, preferred_element_type=f32)
    grad_queries = (
        rotate(grad_query_rot.reshape(length, HEADS, HEAD_DIM), cosine, sine_vals, -1.0)
        .astype(bf16)
        .reshape(length, heads_width)
    )
    grad_keys = (
        rotate(grad_key_rot, cosine, sine_vals, -1.0).astype(bf16).reshape(length, kv_width)
    )
    grad_values_flat = grad_values.reshape(length, kv_width)
    grad_qkv = jnp.concatenate([grad_queries, grad_keys, grad_values_flat], axis=1)
    grad_normed_one = natural(
        tuple(dot(grad_qkv, qkv_parts[j], ((1,), (1,))) for j in range(4)), 1
    )
    grad_back_one, gain_one_g = rms_backward(grad_normed_one, scaled_one, inverse_one, gain_one)
    tokens_grad = (grad_middle + grad_back_one).astype(bf16)
    gain_grads = jnp.stack([gain_one_g, gain_two_g], axis=1)
    gain_grads = jnp.pad(gain_grads, ((0, 0), (0, 126))).astype(bf16)

    def qkv_piece(j):
        grads = dot(normed_chunks[j], grad_qkv, ((0,), (0,))).astype(bf16)
        gains_piece = lax.dynamic_slice_in_dim(gain_grads, (own ^ j) * chunk, chunk, 0)
        return jnp.concatenate([grads, gains_piece], axis=1)

    qkv_g = summed(scatter_parts(tuple(qkv_piece(j) for j in range(4))), orders[0])
    wide = heads_width + kv_width
    return (
        mixed,
        tokens_grad,
        qkv_g[:, :heads_width],
        qkv_g[:, heads_width:wide],
        qkv_g[:, wide : wide + kv_width],
        output_g,
        qkv_g[:, wide + kv_width],
        qkv_g[:, wide + kv_width + 1],
        gate_g,
        up_g,
        down_g,
    )


def solution(mesh):
    placed = (
        P(("replica", "shard"), None),
        P("shard", None),
        P("shard", None),
        P("shard", None),
        P("shard", None),
        P("shard"),
        P("shard"),
        P("shard", None, None),
        P("shard", None, None),
        P("shard", None, None),
        P(("replica", "shard"), None),
        P(("replica", "shard"), None),
        P(("replica", "shard"), None),
    )
    return jax.shard_map(
        functools.partial(body, mesh.shape["replica"]),
        mesh=mesh,
        in_specs=placed,
        out_specs=(
            P(("replica", "shard"), None),
            P(("replica", "shard"), None),
            P("shard", None),
            P("shard", None),
            P("shard", None),
            P("shard", None),
            P("shard"),
            P("shard"),
            P("shard", None, None),
            P("shard", None, None),
            P("shard", None, None),
        ),
        check_vma=False,
    )
```

```python
import functools

import jax
import jax.numpy as jnp
from jax import lax
from jax.experimental import pallas as pl
from jax.experimental.pallas import tpu as pltpu
from jax.sharding import PartitionSpec as P

HEADS = 24
KV_HEADS = 8
HEAD_DIM = 64
EXPERTS = 8
TOP_K = 4

EPSILON = 1e-06
SCORE_SCALE = 0.015625
ROPE_BASE = 10000.0
NEGATIVE = -1e30

VMEM_LIMIT = 56 * 1024 * 1024
PAD = 128


def rope_tables(length):
    halfdim = HEAD_DIM // 2
    exponent = jnp.arange(halfdim, dtype=jnp.float32) * (2.0 / HEAD_DIM)
    inverse = ROPE_BASE ** (-exponent)
    angles = jnp.arange(length, dtype=jnp.float32)[:, None] * inverse[None, :]
    cosine, sine = jnp.cos(angles), jnp.sin(angles)
    return (
        jnp.concatenate([cosine] * 4, axis=1),
        jnp.concatenate([-sine, sine] * 2, axis=1),
    )


def mm(a, b, da=1, db=0):
    return lax.dot_general(a, b, (((da,), (db,)), ((), ())), preferred_element_type=jnp.float32)


def kernel_params():
    return pltpu.CompilerParams(vmem_limit_bytes=VMEM_LIMIT)


def cost(microseconds):
    return pl.CostEstimate(
        flops=int(microseconds * 1e9), bytes_accessed=1 << 20, transcendentals=0
    )


def shape(dims, dtype=jnp.bfloat16):
    return jax.ShapeDtypeStruct(dims, dtype)


def whole(array):
    return pl.BlockSpec(array.shape, lambda *_: (0,) * len(array.shape))


def turn(value, cosine, sine):
    lane = lax.broadcasted_iota(jnp.int32, value.shape, 1)
    partner = jnp.where(
        lane % HEAD_DIM < HEAD_DIM // 2,
        pltpu.roll(value, 128 - HEAD_DIM // 2, 1),
        pltpu.roll(value, HEAD_DIM // 2, 1),
    )
    return value * cosine + partner * sine


def halves(value):
    lane = lax.broadcasted_iota(jnp.int32, value.shape, 1)
    low = lane < HEAD_DIM
    zero = jnp.zeros_like(value)
    swapped = pltpu.roll(value.astype(jnp.float32), HEAD_DIM, 1).astype(value.dtype)
    return (
        (jnp.where(low, value, zero), jnp.where(low, zero, swapped)),
        (jnp.where(low, swapped, zero), jnp.where(low, zero, value)),
    )


def gain_row(gain_ref, own, which):
    return jnp.concatenate(
        [gain_ref[own ^ n, which : which + 1, :] for n in range(4)], axis=1
    ).astype(jnp.float32)


def attend_kernel(
    own_ref, tokens_ref, gain_ref, cos_ref, sin_ref,
    wq0, wq1, wq2, wq3, wk0, wk1, wk2, wk3, wv0, wv1, wv2, wv3,
    norm_ref, q_ref, k_ref, v_ref, att_ref, log_ref,
):
    own = own_ref[0]
    length, width = tokens_ref.shape
    chunk = width // 4

    @pl.when(pl.program_id(0) == 0)
    def _():
        x = tokens_ref[...].astype(jnp.float32)
        inverse = lax.rsqrt(jnp.mean(x * x, axis=1, keepdims=True) + EPSILON)
        normed = (x * inverse * gain_row(gain_ref, own, 0)).astype(jnp.bfloat16)
        for n in range(4):
            norm_ref[n] = normed[:, n * chunk : (n + 1) * chunk]

    parts = [norm_ref[own ^ j] for j in range(4)]

    def project(weights):
        total = mm(parts[0], weights[0][...])
        for j in range(1, 4):
            total = total + mm(parts[j], weights[j][...])
        return total

    query = project((wq0, wq1, wq2, wq3))
    key = project((wk0, wk1, wk2, wk3))
    value = project((wv0, wv1, wv2, wv3)).astype(jnp.bfloat16)
    cosine, sine = cos_ref[...], sin_ref[...]
    key = turn(key, cosine, sine).astype(jnp.bfloat16)
    k_ref[...] = key
    v_ref[...] = value
    keys, values = halves(key), halves(value)
    row = lax.broadcasted_iota(jnp.int32, (length, length), 0)
    col = lax.broadcasted_iota(jnp.int32, (length, length), 1)
    allowed = row >= col
    for b in range(3):
        q = turn(query[:, b * 128 : (b + 1) * 128], cosine, sine).astype(jnp.bfloat16)
        q_ref[0, :, b * 128 : (b + 1) * 128] = q
        total = None
        for half in range(2):
            group = (2 * b + half) // 3
            scores = jnp.where(allowed, mm(q, keys[group][half], 1, 1) * SCORE_SCALE, NEGATIVE)
            top = jnp.max(scores, axis=1, keepdims=True)
            grown = jnp.exp(scores - top)
            size = jnp.sum(grown, axis=1, keepdims=True)
            probs = (grown * (1.0 / size)).astype(jnp.bfloat16)
            head = 2 * b + half
            log_ref[0, :, head : head + 1] = top + jnp.log(size)
            part = mm(probs, values[group][half])
            total = part if total is None else total + part
        att_ref[0, :, b * 128 : (b + 1) * 128] = total.astype(jnp.bfloat16)


def attend(own, tokens, gains, cosine, sine, qkv):
    length, width = tokens.shape
    chunk = width // 4
    kv = KV_HEADS * HEAD_DIM // 4
    return pl.pallas_call(
        attend_kernel,
        grid_spec=pltpu.PrefetchScalarGridSpec(
            num_scalar_prefetch=1,
            grid=(4,),
            in_specs=[whole(tokens), whole(gains), whole(cosine), whole(sine)]
            + projection_specs(qkv, width),
            out_specs=[
                pl.BlockSpec((4, length, chunk), lambda n, own: (0, 0, 0)),
                pl.BlockSpec((1, length, chunk), lambda n, own: (n, 0, 0)),
                pl.BlockSpec((length, kv), lambda n, own: (0, n)),
                pl.BlockSpec((length, kv), lambda n, own: (0, n)),
                pl.BlockSpec((1, length, chunk), lambda n, own: (n, 0, 0)),
                pl.BlockSpec((1, length, PAD), lambda n, own: (n, 0, 0)),
            ],
        ),
        out_shape=[
            shape((4, length, chunk)),
            shape((4, length, chunk)),
            shape((length, 4 * kv)),
            shape((length, 4 * kv)),
            shape((4, length, chunk)),
            shape((4, length, PAD), jnp.float32),
        ],
        compiler_params=kernel_params(),
        cost_estimate=cost(18),
        name="attend",
    )(own, tokens, gains, cosine, sine, *qkv, *qkv, *qkv)


def projection_specs(qkv, width):
    rows = qkv[0].shape[0]
    chunk, kv = width // 4, KV_HEADS * HEAD_DIM // 4
    key, value = width // kv, width // kv + 4
    return (
        [pl.BlockSpec((rows, chunk), lambda n, own: (0, n))] * 4
        + [pl.BlockSpec((rows, kv), lambda n, own: (0, key + n))] * 4
        + [pl.BlockSpec((rows, kv), lambda n, own: (0, value + n))] * 4
    )


def middle_kernel(own_ref, tokens_ref, gain_ref, att_ref, w0, w1, w2, w3, mid_ref, norm_ref):
    own = own_ref[0]
    total = tokens_ref[...].astype(jnp.float32)
    for j, w in enumerate((w0, w1, w2, w3)):
        total = total + mm(att_ref[own ^ j], w[...])
    mid_ref[...] = total
    inverse = lax.rsqrt(jnp.mean(total * total, axis=1, keepdims=True) + EPSILON)
    norm_ref[...] = (total * inverse * gain_row(gain_ref, own, 1)).astype(jnp.bfloat16)


def middle_of(own, tokens, gains, att, wo):
    length, width = tokens.shape
    rows = length // 3
    return pl.pallas_call(
        middle_kernel,
        grid_spec=pltpu.PrefetchScalarGridSpec(
            num_scalar_prefetch=1,
            grid=(3,),
            in_specs=[
                pl.BlockSpec((rows, width), lambda i, own: (i, 0)),
                whole(gains),
                pl.BlockSpec((4, rows, width // 4), lambda i, own: (0, i, 0)),
            ]
            + [whole(a) for a in wo],
            out_specs=[
                pl.BlockSpec((rows, width), lambda i, own: (i, 0)),
                pl.BlockSpec((rows, width), lambda i, own: (i, 0)),
            ],
        ),
        out_shape=[
            jax.ShapeDtypeStruct((length, width), jnp.float32),
            jax.ShapeDtypeStruct((length, width), jnp.bfloat16),
        ],
        compiler_params=kernel_params(),
        cost_estimate=cost(7),
        name="middle",
    )(own, tokens, gains, att, *wo)


def back_two_kernel(
    own_ref, first_ref, near_ref, far_ref, mid_ref, gain_ref, cot_ref, att_ref, w0, w1, w2, w3,
    gm_ref, ga_ref, keep_ref, send_ref, gg_ref,
):
    own = own_ref[0]
    chunk = att_ref.shape[2]
    grad_normed = (
        first_ref[...].astype(jnp.float32)
        + near_ref[...].astype(jnp.float32)
        + far_ref[...].astype(jnp.float32)
    )
    middle = mid_ref[...]
    inverse = lax.rsqrt(jnp.mean(middle * middle, axis=1, keepdims=True) + EPSILON)
    scaled = middle * inverse
    gains = jnp.sum(grad_normed * scaled, axis=0, keepdims=True)
    for n in range(4):
        gg_ref[n] = jnp.broadcast_to(gains[:, n * chunk : (n + 1) * chunk], (8, chunk))
    grad_scaled = grad_normed * gain_row(gain_ref, own, 1)
    inner = jnp.mean(grad_scaled * scaled, axis=1, keepdims=True)
    grad_middle = cot_ref[...].astype(jnp.float32) + inverse * (grad_scaled - scaled * inner)
    gm_ref[...] = grad_middle
    rounded = grad_middle.astype(jnp.bfloat16)
    for j, w in enumerate((w0, w1, w2, w3)):
        ga_ref[own ^ j] = mm(rounded, w[...], 1, 1).astype(jnp.bfloat16)
        target = send_ref if j % 2 else keep_ref
        target[j // 2] = mm(att_ref[own ^ j], rounded, 0, 0).astype(jnp.bfloat16)


def back_two(own, first, near, far, mid, gains, cot, att, wo):
    length, width = mid.shape
    args = (first, near, far, mid, gains, cot, att) + tuple(wo)
    return pl.pallas_call(
        back_two_kernel,
        in_specs=[pl.BlockSpec(memory_space=pltpu.SMEM)]
        + [pl.BlockSpec(memory_space=pltpu.VMEM)] * len(args),
        out_specs=[pl.BlockSpec(memory_space=pltpu.VMEM)] * 5,
        out_shape=[
            shape((length, width), jnp.float32),
            shape((4, length, width // 4)),
            shape((2, width // 4, width)),
            shape((2, width // 4, width)),
            shape((4, 8, width // 4), jnp.float32),
        ],
        compiler_params=kernel_params(),
        cost_estimate=cost(13),
        name="back_two",
    )(own, *args)


def back_one_kernel(
    own_ref, q_ref, k_ref, v_ref, att_ref, ga_ref, log_ref, cos_ref, sin_ref,
    norm_ref, tokens_ref, gain_ref, gm_ref, gtwo_ref,
    wq0, wq1, wq2, wq3, wk0, wk1, wk2, wk3, wv0, wv1, wv2, wv3,
    keep_ref, send_ref, tg_ref, acc_ref, gains_ref,
):
    own = own_ref[0]
    step = pl.program_id(0)
    length = k_ref.shape[0]
    chunk = q_ref.shape[2]

    keys, values = halves(k_ref[...]), halves(v_ref[...])
    cosine, sine = cos_ref[...], -sin_ref[...]
    row = lax.broadcasted_iota(jnp.int32, (length, length), 0)
    col = lax.broadcasted_iota(jnp.int32, (length, length), 1)
    lane = lax.broadcasted_iota(jnp.int32, (length, 128), 1)
    lows = lane < HEAD_DIM
    grad_keys = jnp.zeros((length, 128), jnp.float32)
    grad_values = jnp.zeros((length, 128), jnp.float32)
    grad_query = []
    for b in range(3):
        lanes = slice(b * 128, (b + 1) * 128)
        q = q_ref[0, :, lanes]
        ga = ga_ref[0, :, lanes]
        prod = ga.astype(jnp.float32) * att_ref[0, :, lanes].astype(jnp.float32)
        total = None
        for half in range(2):
            h = 2 * b + half
            group = h // 3
            keep = lows if half == 0 else jnp.logical_not(lows)
            delta = jnp.sum(jnp.where(keep, prod, 0.0), axis=1, keepdims=True)
            kh, vh = keys[group][half], values[group][half]
            scores = mm(q, kh, 1, 1) * SCORE_SCALE
            probs = jnp.where(row >= col, jnp.exp(scores - log_ref[0, :, h : h + 1]), 0.0)
            grad_probs = mm(ga, vh, 1, 1)
            grad_scores = (probs * (grad_probs - delta) * SCORE_SCALE).astype(jnp.bfloat16)
            part = mm(grad_scores, kh)
            total = part if total is None else total + part
            gk = mm(grad_scores, q, 0, 0)
            gv = mm(probs.astype(jnp.bfloat16), ga, 0, 0)
            gk = jnp.where(keep, gk, 0.0)
            gv = jnp.where(keep, gv, 0.0)
            if half != group:
                gk = pltpu.roll(gk, HEAD_DIM, 1)
                gv = pltpu.roll(gv, HEAD_DIM, 1)
            grad_keys = grad_keys + gk
            grad_values = grad_values + gv
        grad_query.append(turn(total, cosine, sine).astype(jnp.bfloat16))
    gq = jnp.concatenate(grad_query, axis=1)
    gk = turn(grad_keys, cosine, sine).astype(jnp.bfloat16)
    gv = grad_values.astype(jnp.bfloat16)

    @pl.when(step == 0)
    def _():
        acc_ref[...] = jnp.zeros_like(acc_ref)

    weights = ((wq0, wk0, wv0), (wq1, wk1, wv1), (wq2, wk2, wv2), (wq3, wk3, wv3))
    for j in range(4):
        wq, wk, wv = weights[j]
        acc_ref[own ^ j] += (
            mm(gq, wq[...], 1, 1) + mm(gk, wk[...], 1, 1) + mm(gv, wv[...], 1, 1)
        )
        normed = norm_ref[own ^ j]
        target = send_ref if j % 2 else keep_ref
        grads = mm(normed, jnp.concatenate([gq, gk, gv], axis=1), 0, 0).astype(jnp.bfloat16)
        for start, size, at in (
            (0, chunk, 0),
            (chunk, 128, 4 * chunk),
            (chunk + 128, 128, 4 * chunk + 512),
        ):
            place = pl.ds(pl.multiple_of(at + step * size, 128), size)
            target[j // 2, :, place] = grads[:, start : start + size]

    @pl.when(step == pl.num_programs(0) - 1)
    def _():
        x = tokens_ref[...].astype(jnp.float32)
        inverse = lax.rsqrt(jnp.mean(x * x, axis=1, keepdims=True) + EPSILON)
        gain_one = gain_row(gain_ref, own, 0)
        gains_ref[...] = jnp.zeros_like(gains_ref)
        inner = jnp.zeros((length, 1), jnp.float32)
        for n in range(4):
            lanes = slice(n * chunk, (n + 1) * chunk)
            scaled = tokens_ref[:, lanes].astype(jnp.float32) * inverse
            grad_normed = acc_ref[n]
            gains_ref[n, 0:1, :] = jnp.sum(grad_normed * scaled, axis=0, keepdims=True)
            gains_ref[n, 1:2, :] = gtwo_ref[n, 0:1, :]
            grad_scaled = grad_normed * gain_one[:, lanes]
            acc_ref[n] = grad_scaled
            inner = inner + jnp.sum(grad_scaled * scaled, axis=1, keepdims=True)
        inner = inner * (1.0 / (4 * chunk))
        for n in range(4):
            lanes = slice(n * chunk, (n + 1) * chunk)
            scaled = tokens_ref[:, lanes].astype(jnp.float32) * inverse
            tg_ref[:, lanes] = (
                gm_ref[:, lanes] + inverse * (acc_ref[n] - scaled * inner)
            ).astype(jnp.bfloat16)
        across = lax.broadcasted_iota(jnp.int32, (chunk, chunk), 0)
        down = lax.broadcasted_iota(jnp.int32, (chunk, chunk), 1)
        identity = jnp.where(across == down, 1.0, 0.0).astype(jnp.bfloat16)
        wide = keep_ref.shape[2]
        for j in range(4):
            target = send_ref if j % 2 else keep_ref
            rows = gains_ref[own ^ j].astype(jnp.bfloat16)
            target[j // 2, :, wide - PAD : wide] = mm(identity, rows, 1, 1).astype(jnp.bfloat16)


def back_one(own, q, k, v, att, ga, log, cosine, sine, norm, tokens, gains, gm, gtwo, qkv):
    length, width = tokens.shape
    chunk = width // 4
    kv = k.shape[1] // 4
    wide = width + 8 * kv + PAD
    cols = lambda a: pl.BlockSpec((a.shape[0], a.shape[1] // 4), lambda n, own: (0, n))
    lead = lambda a: pl.BlockSpec((1,) + a.shape[1:], lambda n, own: (n, 0, 0))
    return pl.pallas_call(
        back_one_kernel,
        grid_spec=pltpu.PrefetchScalarGridSpec(
            num_scalar_prefetch=1,
            grid=(4,),
            in_specs=[lead(q), cols(k), cols(v), lead(att), lead(ga), lead(log)]
            + [whole(a) for a in (cosine, sine, norm, tokens, gains, gm, gtwo)]
            + projection_specs(qkv, width),
            out_specs=[
                pl.BlockSpec((2, chunk, wide), lambda n, own: (0, 0, 0)),
                pl.BlockSpec((2, chunk, wide), lambda n, own: (0, 0, 0)),
                pl.BlockSpec((length, width), lambda n, own: (0, 0)),
            ],
            scratch_shapes=[
                pltpu.VMEM((4, length, chunk), jnp.float32),
                pltpu.VMEM((4, PAD, chunk), jnp.float32),
            ],
        ),
        out_shape=[shape((2, chunk, wide)), shape((2, chunk, wide)), shape((length, width))],
        compiler_params=kernel_params(),
        cost_estimate=cost(36),
        name="back_one",
    )(own, q, k, v, att, ga, log, cosine, sine, norm, tokens, gains, gm, gtwo, *qkv, *qkv, *qkv)


def experts_kernel(
    n0, n1, g0, g1, row_ref, gate_ref, up_ref, down_ref,
    x_ref, gr_ref, h_ref, gg_ref, gu_ref, moe0_ref, moe1_ref, gn0_ref, gn1_ref, moe_acc, gn_acc,
):
    q, e = pl.program_id(0), pl.program_id(1)
    cap = x_ref.shape[2]
    length = n0.shape[0]
    slot_row, prob_row = row_ref[0, 0, 0:1, :], row_ref[0, 0, 1:2, :]
    slots = lax.broadcasted_iota(jnp.int32, (cap, length), 0).astype(jnp.float32)
    hit = slots == slot_row
    prob = jnp.sum(jnp.where(hit, prob_row, 0.0), axis=1, keepdims=True)
    pick = jnp.where(hit, 1.0, 0.0).astype(jnp.bfloat16)

    def fetch(n, g):
        x_ref[0, 0] = mm(pick, n[...]).astype(jnp.bfloat16)
        gr_ref[0, 0] = (mm(pick, g[...]) * prob).astype(jnp.bfloat16)

    pl.when(q == 0)(lambda: fetch(n0, g0))
    pl.when(q == 1)(lambda: fetch(n1, g1))
    x = x_ref[0, 0]
    gr = gr_ref[0, 0]
    gate, up, down = gate_ref[0], up_ref[0], down_ref[0]
    gate_pre = mm(x, gate)
    up_pre = mm(x, up)
    sig = jax.nn.sigmoid(gate_pre)
    act = gate_pre * sig
    hidden = (act * up_pre).astype(jnp.bfloat16)
    h_ref[0, 0] = hidden
    grad_hidden = mm(gr, down, 1, 1)
    grad_up = (grad_hidden * act).astype(jnp.bfloat16)
    grad_gate = (grad_hidden * up_pre * sig * (1.0 + gate_pre * (1.0 - sig))).astype(jnp.bfloat16)
    gu_ref[0, 0] = grad_up
    gg_ref[0, 0] = grad_gate
    result = (mm(hidden, down) * prob).astype(jnp.bfloat16)
    grad_buffers = (mm(grad_gate, gate, 1, 1) + mm(grad_up, up, 1, 1)).astype(jnp.bfloat16)
    moe = mm(pick, result, 0, 0)
    gn = mm(pick, grad_buffers, 0, 0)
    last = pl.num_programs(1) - 1

    @pl.when(e == 0)
    def _():
        moe_acc[...] = moe
        gn_acc[...] = gn

    @pl.when(e > 0)
    def _():
        moe_acc[...] += moe
        gn_acc[...] += gn

    for turn_of, moe_ref, gn_ref in ((0, moe0_ref, gn0_ref), (1, moe1_ref, gn1_ref)):

        @pl.when((e == last) & (q == turn_of))
        def _():
            moe_ref[...] = moe_acc[...].astype(jnp.bfloat16)
            gn_ref[...] = gn_acc[...].astype(jnp.bfloat16)


def experts(n0, n1, g0, g1, row, gate, up, down, cap):
    length, width = n0.shape
    held, _, ff = gate.shape
    tok = pl.BlockSpec((1, 1, cap, width), lambda q, e: (e, q, 0, 0))
    hid = pl.BlockSpec((1, 1, cap, ff), lambda q, e: (e, q, 0, 0))
    return pl.pallas_call(
        experts_kernel,
        grid=(2, held),
        in_specs=[whole(n0)] * 4
        + [
            pl.BlockSpec((1, 1, 2, length), lambda q, e: (q, e, 0, 0)),
            pl.BlockSpec((1, width, ff), lambda q, e: (e, 0, 0)),
            pl.BlockSpec((1, width, ff), lambda q, e: (e, 0, 0)),
            pl.BlockSpec((1, ff, width), lambda q, e: (e, 0, 0)),
        ],
        out_specs=[tok, tok, hid, hid, hid] + [whole(n0)] * 4,
        out_shape=[shape((held, 2, cap, width))] * 2
        + [shape((held, 2, cap, ff))] * 3
        + [shape((length, width))] * 4,
        scratch_shapes=[pltpu.VMEM((length, width), jnp.float32)] * 2,
        compiler_params=kernel_params(),
        cost_estimate=cost(26),
        name="experts",
    )(n0, n1, g0, g1, row, gate, up, down)


def wgrad_kernel(which, xa, xb, ga, gb, ua, ub, ha, hb, ra, rb, gate_ref, up_ref, down_ref):
    def both(la, lb, r1, r2):
        rows = la.shape[1] * la.shape[2]
        one = mm(la[0].reshape(rows, la.shape[3]), r1[0].reshape(rows, r1.shape[3]), 0, 0)
        two = mm(lb[0].reshape(rows, lb.shape[3]), r2[0].reshape(rows, r2.shape[3]), 0, 0)
        return (one + two).astype(jnp.bfloat16)

    gate_ref[...] = both(xa, xb, ga, gb)
    up_ref[...] = both(xa, xb, ua, ub)
    down_ref[...] = both(ha, hb, ra, rb)


def wgrad(which, a, b):
    xa, ra, ha, gga, gua = a[:5]
    xb, rb, hb, ggb, gub = b[:5]
    _, two, cap, width = xa.shape
    ff = ha.shape[3]
    steps = 3
    w = width // steps
    tok = pl.BlockSpec((1, two, cap, w), lambda i, which: (which[0], 0, 0, i))
    hid = pl.BlockSpec((1, two, cap, ff), lambda i, which: (which[0], 0, 0, 0))
    return pl.pallas_call(
        wgrad_kernel,
        grid_spec=pltpu.PrefetchScalarGridSpec(
            num_scalar_prefetch=1,
            grid=(steps,),
            in_specs=[tok] * 2 + [hid] * 6 + [tok] * 2,
            out_specs=[pl.BlockSpec((w, ff), lambda i, which: (i, 0))] * 2
            + [pl.BlockSpec((ff, w), lambda i, which: (0, i))],
        ),
        out_shape=[shape((width, ff))] * 2 + [shape((ff, width))],
        compiler_params=kernel_params(),
        cost_estimate=cost(8),
        name="wgrad",
    )(which, xa, xb, gga, ggb, gua, gub, ha, hb, ra, rb)


def after(value, *others):
    return lax.optimization_barrier((value,) + others)[0]


def neighbour_core(value):
    return lax.ppermute(value, "shard", [(0, 1), (1, 0), (2, 3), (3, 2)])


def neighbour_x(value):
    return lax.ppermute(value, "shard", [(0, 2), (2, 0), (1, 3), (3, 1)])


def add(a, b):
    return (a.astype(jnp.float32) + b.astype(jnp.float32)).astype(jnp.bfloat16)


class Replicas:
    def __init__(self, count):
        self.count = count
        self.index = lax.axis_index("replica")

    def bits(self):
        bits, bit = [], 1
        while bit < self.count:
            bits.append(bit)
            bit *= 2
        return bits

    def side(self, bit):
        return jnp.minimum(self.index & bit, 1)

    def flip(self, value, bit):
        return lax.ppermute(value, "replica", [(i, i ^ bit) for i in range(self.count)])

    def half(self, value, which):
        halves = value.reshape((2, value.shape[0] // 2) + value.shape[1:])
        return lax.dynamic_index_in_dim(halves, which, 0, keepdims=False)

    def middle(self, kept, got, order):
        trail = []
        for bit in order[:-1]:
            mine = self.side(bit)
            sent = add(self.half(kept, 1 - mine), self.half(got, 1 - mine))
            kept, got = (
                add(self.half(kept, mine), self.half(got, mine)),
                self.flip(sent, bit),
            )
            trail.append(bit)
        value = add(kept, got)
        value = add(value, self.flip(value, order[-1]))
        for bit in trail[::-1]:
            value = self.join(value, self.flip(value, bit), bit)
        return value

    def join(self, own, other, bit):
        low = (self.index & bit) == 0
        return jnp.concatenate([jnp.where(low, own, other), jnp.where(low, other, own)], axis=0)

    def total(self, value, order):
        mine = self.side(order[0])
        sent = self.flip(self.half(value, 1 - mine), order[0])
        own = self.middle(self.half(value, mine), sent, order[1:])
        return self.join(own, self.flip(own, order[0]), order[0]).astype(jnp.float32)


def body(
    count,
    tokens,
    query_weight,
    key_weight,
    value_weight,
    output_weight,
    attn_gain,
    moe_gain,
    gate_weight,
    up_weight,
    down_weight,
    routes,
    route_probs,
    cotangent,
):
    f32 = jnp.float32
    bf16 = jnp.bfloat16
    length, model_width = tokens.shape
    capacity = length * 2 // 3
    own = lax.axis_index("shard")
    own_ref = own.reshape(1)
    held = gate_weight.shape[0]
    replicas = Replicas(count)
    bits = replicas.bits()
    orders = (bits, [bits[1], bits[0]] + bits[2:])

    gains_own = jnp.stack([attn_gain, moe_gain])
    gains_x = neighbour_x(gains_own)
    qkv_own = jnp.concatenate([query_weight, key_weight, value_weight], axis=1)
    qkv_x = neighbour_x(qkv_own)
    gains = jnp.stack(
        [gains_own, neighbour_core(gains_own), gains_x, neighbour_core(gains_x)]
    )
    qkv = (qkv_own, neighbour_core(qkv_own), qkv_x, neighbour_core(qkv_x))

    expert_ids = jnp.arange(EXPERTS, dtype=jnp.int32)
    named = routes[:, :, None] == expert_ids[None, None, :]
    taken = jnp.any(named, axis=1)
    prob_of = jnp.sum(jnp.where(named, route_probs[:, :, None], 0.0), axis=1)
    positions = jnp.arange(length)
    before = (positions[:, None] > positions[None, :]).astype(bf16)
    slot_of = jnp.where(taken, mm(before, taken.astype(bf16)), -1.0)
    info_own = jnp.concatenate([slot_of, prob_of], axis=1).T
    info_x = neighbour_x(info_own)
    output_x = neighbour_x(output_weight)
    cotangent_x = neighbour_x(cotangent)

    cosine, sine = rope_tables(length)
    norm_one, q, k, v, att, log = attend(own_ref, tokens, gains, cosine, sine, qkv)
    output_x = after(output_x, att)
    output = (output_weight, neighbour_core(output_weight), output_x, neighbour_core(output_x))
    middle, normed_two = middle_of(own_ref, tokens, gains, att, output)

    def pair(first, second, grad_first, grad_second, info_first, info_second):
        table = jnp.stack([info_first, info_second]).reshape(2, 2, EXPERTS, length)
        table = lax.dynamic_slice_in_dim(table, own * held, held, 2).transpose(0, 2, 1, 3)
        return experts(
            first, second, grad_first, grad_second, table, gate_weight, up_weight, down_weight,
            capacity,
        )

    normed_x = neighbour_x(normed_two)
    near = pair(
        normed_two,
        neighbour_core(normed_two),
        cotangent,
        neighbour_core(cotangent),
        info_own,
        neighbour_core(info_own),
    )
    cotangent_x = after(cotangent_x, middle)
    normed_x = after(normed_x, near[5])
    far = pair(
        normed_x,
        neighbour_core(normed_x),
        cotangent_x,
        neighbour_core(cotangent_x),
        info_x,
        neighbour_core(info_x),
    )
    grad_near = neighbour_core(near[8])
    moe_near = neighbour_core(near[6])
    grad_far = add(far[7], neighbour_core(far[8]))
    grad_far_x = neighbour_x(grad_far)

    bit_a, bit_b = orders[0][0], orders[1][0]
    held_ready = tuple(far[:5])
    held_ready = tuple(lax.optimization_barrier(held_ready + (grad_far,))[:5])
    sends = [wgrad((1 - replicas.side(bit_a)).reshape(1), near, held_ready)]
    got = [replicas.flip(value, bit_a) for value in sends[0]]
    held_ready = tuple(lax.optimization_barrier(held_ready + tuple(sends[0]))[:5])
    keeps = wgrad(replicas.side(bit_a).reshape(1), near, held_ready)

    moe_far = add(far[5], neighbour_core(after(far[6], grad_far)))
    moe_far_x = neighbour_x(after(moe_far, grad_far_x))

    grad_middle, grad_att, og_keep, og_send, gain_two = back_two(
        own_ref, near[7], grad_near, grad_far_x, middle, gains, cotangent, att, output
    )
    og_got = neighbour_core(og_send)
    og_x = neighbour_x(add(og_keep[1], og_got[1]))
    qkv_keep, qkv_send, tokens_grad = back_one(
        own_ref, q, k, v, att, grad_att, log, cosine, sine, norm_one, tokens, gains, grad_middle,
        gain_two, qkv,
    )
    qkv_got = neighbour_core(qkv_send)
    qkv_x = neighbour_x(add(qkv_keep[1], qkv_got[1]))

    def three(a, b, c):
        return (a.astype(f32) + b.astype(f32) + c.astype(f32)).astype(bf16)

    output_g = replicas.total(three(og_keep[0], og_got[0], og_x), orders[1])
    qkv_g = replicas.total(three(qkv_keep[0], qkv_got[0], qkv_x), orders[0])
    mixed = (
        middle + near[5].astype(f32) + moe_near.astype(f32) + moe_far_x.astype(f32)
    ).astype(bf16)

    def finish(kept, value):
        own_half = replicas.middle(kept, value, orders[0][1:])
        full = replicas.join(own_half, replicas.flip(own_half, bit_a), bit_a)
        return full.astype(f32).reshape((held,) + kept.shape)

    gate_g, up_g, down_g = [finish(kept, value) for kept, value in zip(keeps, got)]
    query_end = model_width
    key_end = query_end + key_weight.shape[1]
    value_end = key_end + value_weight.shape[1]
    return (
        mixed,
        tokens_grad,
        qkv_g[:, :query_end],
        qkv_g[:, query_end:key_end],
        qkv_g[:, key_end:value_end],
        output_g,
        qkv_g[:, value_end],
        qkv_g[:, value_end + 1],
        gate_g,
        up_g,
        down_g,
    )


def solution(mesh):
    placed = (
        P(("replica", "shard"), None),
        P("shard", None),
        P("shard", None),
        P("shard", None),
        P("shard", None),
        P("shard"),
        P("shard"),
        P("shard", None, None),
        P("shard", None, None),
        P("shard", None, None),
        P(("replica", "shard"), None),
        P(("replica", "shard"), None),
        P(("replica", "shard"), None),
    )
    return jax.shard_map(
        functools.partial(body, mesh.shape["replica"]),
        mesh=mesh,
        in_specs=placed,
        out_specs=(
            P(("replica", "shard"), None),
            P(("replica", "shard"), None),
            P("shard", None),
            P("shard", None),
            P("shard", None),
            P("shard", None),
            P("shard"),
            P("shard"),
            P("shard", None, None),
            P("shard", None, None),
            P("shard", None, None),
        ),
        check_vma=False,
    )
```
